32 devices in a mesh: rep: 8 (over y, x, core), fsdp: 4 (over z).
Axes of the slice: x: 2, y: 2, z: 4, core: 2. Of those that a mesh axis runs over, the one named last changes fastest.
Arguments:
- block_input: bfloat16 [32, 256, 512], P(('rep', 'fsdp')), may hold values from -6 to 6
- cotangent: bfloat16 [32, 256, 512], P(('rep', 'fsdp')), may hold values from -6 to 6
- seq_valid: int32 [32], P(('rep', 'fsdp')), may hold values 0 or 1
- in_weight: float32 [512, 1536], P('fsdp'), may hold values from -0.25 to 0.25
- out_weight: float32 [512, 512], P('fsdp'), may hold values from -0.75 to 0.75
- small_params: float32 [6914], replicated, may hold values from -8 to 8, as said below
- in_moment: float32 [512, 1536], P('fsdp'), may hold values from -18 to 18
- in_second: float32 [512, 1536], P('fsdp'), may hold values from 1 to 100
- out_moment: float32 [512, 512], P('fsdp'), may hold values from -18 to 18
- out_second: float32 [512, 512], P('fsdp'), may hold values from 1 to 100
- small_moment: float32 [6914], replicated, may hold values from -18 to 18
- small_second: float32 [6914], replicated, may hold values from 1 to 100
Outputs:
- block_output: float32 [32, 256, 512], P(('rep', 'fsdp'))
- input_grad: float32 [32, 256, 512], P(('rep', 'fsdp'))
- in_weight_grad: float32 [512, 1536], P('fsdp')
- out_weight_grad: float32 [512, 512], P('fsdp')
- small_grad: float32 [6914], replicated
- new_in_weight: float32 [512, 1536], P('fsdp')
- new_out_weight: float32 [512, 512], P('fsdp')
- new_small: float32 [6914], replicated
- new_in_moment: float32 [512, 1536], P('fsdp')
- new_in_second: float32 [512, 1536], P('fsdp')
- new_out_moment: float32 [512, 512], P('fsdp')
- new_out_second: float32 [512, 512], P('fsdp')
- new_small_moment: float32 [6914], replicated
- new_small_second: float32 [6914], replicated
The draws below stay inside these ranges and needn't reach their ends.
Inputs may be any that keep to these rules, and one draw needn't show every extreme that they name: `small_params`: entries 512 + 2 * 2 * 512 + 4 (1024) to that plus 2 lie in -4.7 to 0.
All inputs are finite; a program needn't handle non-finite values. No bound on the sum of `seq_valid` on one device may be relied on, other than what follows from the above.
Results may differ from the reference program's by a relative error of at most 0.00105.
The reference program's roundings to bfloat16 on the way (of `in_bf` and `upstream`) count: a program that leaves them out, or rounds other values in their place, can miss the bound.
Values may be sent and summed in bfloat16 or wider, within the bound.
A program may use at most 128 MiB of HBM per device.

```python
import math
import jax
import jax.numpy as jnp
from jax import lax

D = 512
H = 2
DK = 128
DV = 256
CONV = 4
STEP = 3
LEN = 256
SEQS = 32
PROJ = 1536
SMALL = 6914


def draw_small_params(key, part):
    channels = 2 * H * DK + H * DV
    keys = jax.random.split(key, 5)
    gain_in = 1.0 + 0.2 * jax.random.normal(keys[0], (D,), jnp.float32)
    beta_weight = jax.random.normal(keys[1], (D * 2 * H,), jnp.float32) * (3.0 / math.sqrt(D))
    conv_taps = 0.5 * jax.random.normal(keys[2], (CONV * channels,), jnp.float32)
    out_gain = 1.0 + 0.2 * jax.random.normal(keys[4], (DV,), jnp.float32)
    decay_log = jax.random.uniform(keys[3], (H,), jnp.float32, -4.6, 0.0)
    return jnp.concatenate([gain_in, beta_weight, conv_taps, decay_log, out_gain])


def plant(array, own_key, smallest, top_value):
    shape = array.shape
    spot = [jax.random.randint(jax.random.fold_in(own_key, axis), (), 0, shape[axis]) for axis in range(len(shape))]
    array = array.at[tuple(spot)].set(smallest)
    longest = shape.index(max(shape))
    spot[longest] = (spot[longest] + 1) % shape[longest]
    return array.at[tuple(spot)].set(top_value)


def block_scale(stream_key, extent, pieces, low, high):
    factor_of, own = 1.0, jax.random.fold_in(stream_key, 6)
    for axis_at, shards_of in pieces:
        draws = jnp.exp(jax.random.uniform(jax.random.fold_in(own, axis_at), (shards_of,), jnp.float32, low / len(pieces), high / len(pieces)))
        factor_of = factor_of * jnp.repeat(draws, extent[axis_at] // shards_of).reshape([-1 if axis == axis_at else 1 for axis in range(len(extent))])
    return factor_of


def gaussian(stream_key, shape, spread, most, shards=(), held_as=jnp.bfloat16):
    loudness = block_scale(stream_key, shape, shards, -0.22, 0.18) if shards else 1.0
    drawn = jax.random.normal(stream_key, shape, jnp.float32) * spread * loudness
    return jnp.minimum(jnp.maximum(drawn, -most), most).astype(held_as)


def setup_inputs(seed: int = 0) -> dict:
    splits = jax.random.split(jax.random.key(seed), 13)
    block_input = gaussian(splits[0], (SEQS, LEN, D), 1.0, 6.0, ((0, 32),))
    cotangent = gaussian(splits[1], (SEQS, LEN, D), 1.0, 6.0, ((0, 32),))
    seq_valid = plant((jax.random.randint(splits[2], (SEQS,), 0, 8) < 7).astype(jnp.int32), jax.random.fold_in(splits[2], 1), 0, 1)
    in_weight = gaussian(splits[3], (D, PROJ), D ** -0.5, 0.25, ((0, 4),), jnp.float32)
    out_weight = gaussian(splits[4], (H * DV, D), (H * DV // 8) ** -0.5, 0.75, ((0, 4),), jnp.float32)
    small_params = draw_small_params(jax.random.fold_in(splits[12], 71), 0)
    in_moment = gaussian(splits[6], (D, PROJ), 3.0, 18.0, ((0, 4),), jnp.float32)
    in_second = jnp.clip(jnp.exp(math.log(100.0) - 4.6051702 * jax.random.uniform(splits[7], (D, PROJ), jnp.float32) ** block_scale(splits[7], (D, PROJ), ((0, 4),), -0.2, 0.2)), 1.0, 100.0)
    out_moment = gaussian(splits[8], (H * DV, D), 3.0, 18.0, ((0, 4),), jnp.float32)
    out_second = jnp.clip(jnp.exp(math.log(100.0) - 4.6051702 * jax.random.uniform(splits[9], (H * DV, D), jnp.float32) ** block_scale(splits[9], (H * DV, D), ((0, 4),), -0.2, 0.2)), 1.0, 100.0)
    small_moment = gaussian(splits[10], (SMALL,), 3.0, 18.0, (), jnp.float32)
    small_second = jnp.clip(jnp.exp(jax.random.uniform(splits[11], (SMALL,), jnp.float32, math.log(1.0), math.log(100.0))), 1.0, 100.0)
    return {"block_input": block_input, "cotangent": cotangent, "seq_valid": seq_valid, "in_weight": in_weight, "out_weight": out_weight, "small_params": small_params, "in_moment": in_moment, "in_second": in_second, "out_moment": out_moment, "out_second": out_second, "small_moment": small_moment, "small_second": small_second}


EPS_NORM = 1e-06
BETA_ONE = 0.9
BETA_TWO = 0.95
ADAM_EPS = 1e-08
LEARN_RATE = 0.01
WEIGHT_DECAY = 0.1
HIGHEST_ACCURACY = lax.Precision.HIGHEST

def split_small(small):
    channels = 2 * H * DK + H * DV
    first = D
    second = first + D * 2 * H
    third = second + CONV * channels
    fourth = third + H
    return (small[:first], small[first:second].reshape(D, 2 * H), small[second:third].reshape(CONV, channels), small[third:fourth], small[fourth:])

def rms_gain(values, gain):
    return values * lax.rsqrt(lax.optimization_barrier(jnp.mean(values * values, axis=-1, keepdims=True)) + EPS_NORM) * gain

def features(projected, beta_gate, conv_taps, decay_log):
    channels = 2 * H * DK + H * DV
    length = projected.shape[0]
    padded = jnp.pad(projected[:, :channels], ((CONV - 1, 0), (0, 0)))
    convolved = conv_taps[0] * padded[0:length]
    for tap in range(1, CONV):
        convolved = convolved + conv_taps[tap] * padded[tap:tap + length]
    activated = jax.nn.silu(convolved)
    queries = activated[:, :H * DK].reshape(length, H, DK)
    key_rows = activated[:, H * DK:2 * H * DK].reshape(length, H, DK)
    values = activated[:, 2 * H * DK:].reshape(length, H, DV)
    queries = queries * lax.rsqrt(lax.optimization_barrier(jnp.sum(queries * queries, axis=-1, keepdims=True)) + EPS_NORM) * DK ** (-0.5)
    key_rows = key_rows * lax.rsqrt(lax.optimization_barrier(jnp.sum(key_rows * key_rows, axis=-1, keepdims=True)) + EPS_NORM)
    betas = jax.nn.sigmoid(beta_gate[:, :H])
    log_decay = -jnp.exp(decay_log) * jax.nn.softplus(beta_gate[:, H:])
    return (queries, key_rows, values, betas, log_decay)

def finish(state_out, projected, out_gain):
    channels = 2 * H * DK + H * DV
    length = projected.shape[0]
    gate_part = projected[:, channels:].reshape(length, H, DV)
    return (rms_gain(state_out, out_gain) * jax.nn.silu(gate_part)).reshape(length, H * DV)

def recurrent(queries, key_rows, values, betas, log_decay):

    def one_step(memory_state, inputs):
        query_token_row, key_token_row, value_token_row, beta_token_row, decay_row = inputs
        memory_state = memory_state * jnp.exp(decay_row)[:, None, None]
        predicted_value = jnp.einsum('pt,ptj->pj', key_token_row, memory_state, precision=HIGHEST_ACCURACY)
        memory_state = memory_state + jnp.einsum('zi,zs->zis', key_token_row, beta_token_row[:, None] * (value_token_row - predicted_value), precision=HIGHEST_ACCURACY)
        return (memory_state, jnp.einsum('pt,ptj->pj', query_token_row, memory_state, precision=HIGHEST_ACCURACY))
    initial = jnp.zeros((H, DK, DV), jnp.float32)
    _, outputs = lax.scan(one_step, initial, (queries, key_rows, values, betas, log_decay))
    return outputs

def mixer_ref(projected, beta_gate, conv_taps, decay_log, out_gain):
    parts = features(projected, beta_gate, conv_taps, decay_log)
    return finish(recurrent(*parts), projected, out_gain)

def adamw(weight, grad, moment, second):
    moment_new = BETA_ONE * moment + (1.0 - BETA_ONE) * grad
    second_new = BETA_TWO * second + (1.0 - BETA_TWO) * grad * grad
    update = moment_new / (1.0 - BETA_ONE ** STEP) / (jnp.sqrt(second_new / (1.0 - BETA_TWO ** STEP)) + ADAM_EPS)
    return (weight - LEARN_RATE * (update + WEIGHT_DECAY * weight), moment_new, second_new)

def reference(block_input, cotangent, seq_valid, in_weight, out_weight, small_params, in_moment, in_second, out_moment, out_second, small_moment, small_second):
    gain_in, beta_weight, conv_taps, decay_log, out_gain = split_small(small_params)
    in_bf = in_weight.astype(jnp.bfloat16)
    out_bf = out_weight.astype(jnp.bfloat16)

    def per_sequence(totals, inputs):
        rows, upstream_raw, flag = inputs
        rows_f = rows.astype(jnp.float32)
        normed = rms_gain(rows_f, gain_in)
        normed_bf = normed.astype(jnp.bfloat16)
        projected = jnp.dot(normed_bf, in_bf, preferred_element_type=jnp.float32)
        beta_gate = jnp.dot(normed, beta_weight, precision=HIGHEST_ACCURACY)
        mixed, mixer_back = jax.vjp(mixer_ref, projected, beta_gate, conv_taps, decay_log, out_gain)
        mixed_bf = mixed.astype(jnp.bfloat16)
        output = rows_f + jnp.dot(mixed_bf, out_bf, preferred_element_type=jnp.float32)
        upstream = upstream_raw * flag.astype(jnp.bfloat16)
        d_mixed = jnp.dot(upstream, out_bf.T, preferred_element_type=jnp.float32)
        d_proj, d_beta, d_conv, d_decay, d_gain_out = mixer_back(d_mixed)
        d_proj_bf = d_proj.astype(jnp.bfloat16)
        d_normed = jnp.dot(d_proj_bf, in_bf.T, preferred_element_type=jnp.float32) + jnp.dot(d_beta, beta_weight.T, precision=HIGHEST_ACCURACY)
        _, norm_back = jax.vjp(rms_gain, rows_f, gain_in)
        d_rows, d_gain_in = norm_back(d_normed)
        grad_in = jnp.dot(normed_bf.T, d_proj_bf, preferred_element_type=jnp.float32)
        grad_out = jnp.dot(mixed_bf.T, upstream, preferred_element_type=jnp.float32)
        small_local = jnp.concatenate([d_gain_in, jnp.dot(normed.T, d_beta, precision=HIGHEST_ACCURACY).reshape(-1), d_conv.reshape(-1), d_decay, d_gain_out])
        totals = (totals[0] + grad_in, totals[1] + grad_out, totals[2] + small_local)
        return (totals, (output, upstream.astype(jnp.float32) + d_rows))
    start_totals = (jnp.zeros(in_weight.shape, jnp.float32), jnp.zeros(out_weight.shape, jnp.float32), jnp.zeros(small_params.shape, jnp.float32))
    totals, (block_output, input_grad) = lax.scan(per_sequence, start_totals, (block_input, cotangent, seq_valid))
    in_grad, out_grad, small_grad = totals
    new_in, in_m, in_v = adamw(in_weight, in_grad, in_moment, in_second)
    new_out, out_m, out_v = adamw(out_weight, out_grad, out_moment, out_second)
    new_small, small_m, small_v = adamw(small_params, small_grad, small_moment, small_second)
    return (block_output, input_grad, in_grad, out_grad, small_grad, new_in, new_out, new_small, in_m, in_v, out_m, out_v, small_m, small_v)
```

```python
import functools

import jax
import jax.numpy as jnp
from jax import lax
from jax.experimental import pallas as pl
from jax.experimental.pallas import tpu as pltpu
from jax.sharding import PartitionSpec as P

D = 512
H = 2
DK = 128
DV = 256
CONV = 4
CHUNK = 128
STEP = 3


EPS_NORM = 1e-06
BETA_ONE = 0.9
BETA_TWO = 0.95
ADAM_EPS = 1e-08
LEARN_RATE = 0.01
WEIGHT_DECAY = 0.1


def split_small(small):
    channels = 2 * H * DK + H * DV
    first = D
    second = first + D * 2 * H
    third = second + CONV * channels
    fourth = third + H
    return (
        small[:first],
        small[first:second].reshape(D, 2 * H),
        small[second:third].reshape(CONV, channels),
        small[third:fourth],
        small[fourth:],
    )


def split(value):
    high = value.astype(jnp.bfloat16)
    return (high, (value - high.astype(jnp.float32)).astype(jnp.bfloat16))


def dot(left, right, left_dim=1, right_dim=0):
    return lax.dot_general(
        left,
        right,
        (((left_dim,), (right_dim,)), ((), ())),
        preferred_element_type=jnp.float32,
    )


def dot3(left, right, left_dim=1, right_dim=0):
    return (
        dot(left[0], right[1], left_dim, right_dim)
        + dot(left[1], right[0], left_dim, right_dim)
    ) + dot(left[0], right[0], left_dim, right_dim)


def row_sum(value):
    return jnp.sum(value, axis=1, keepdims=True)


def col_sum(value):
    return jnp.sum(value, axis=0, keepdims=True)


def sigmoid(value):
    return 1.0 / (1.0 + jnp.exp(-value))


def total(*terms):
    out = None
    for term in terms:
        if term is not None:
            out = term if out is None else out + term
    return out


def unit_inverse(strict, levels, level_masks):
    size = strict[0].shape[0]
    rows = lax.broadcasted_iota(jnp.int32, (size, size), 0)
    cols = lax.broadcasted_iota(jnp.int32, (size, size), 1)
    eye = jnp.where(rows == cols, 1.0, 0.0)
    inverses = [eye - jnp.where(level_masks[0], a, 0.0) for a in strict]
    for level in range(1, levels):
        for n, a in enumerate(strict):
            inv = split(inverses[n])
            inner = dot3(inv, split(jnp.where(level_masks[level], a, 0.0)))
            inverses[n] = inverses[n] - dot3(split(inner), inv)
    return inverses


def local_kernel(
    flag_ref,
    x_ref,
    cot_ref,
    win_ref,
    wout_ref,
    gain_ref,
    bw_ref,
    taps_ref,
    dlog_ref,
    ogain_ref,
    out_ref,
    xgrad_ref,
    gin_ref,
    gout_ref,
    dgain_ref,
    dbw_ref,
    dtaps_ref,
    ddlog_ref,
    dogain_ref,
    proj_ref,
    conv_ref,
    mixed_ref,
    dproj_ref,
    dact_ref,
    *,
    seqs,
):
    f32, bf16 = jnp.float32, jnp.bfloat16
    length, width = x_ref.shape[1:]
    channels = taps_ref.shape[1]
    lanes = bw_ref.shape[1]
    chunk = CHUNK if length % CHUNK == 0 else length
    chunks = length // chunk

    def keep(ref, value):
        if seqs == 1:
            ref[...] = value
        else:

            @pl.when(pl.program_id(0) == 0)
            def _():
                ref[...] = value

            @pl.when(pl.program_id(0) > 0)
            def _():
                ref[...] = ref[...] + value

    gain = gain_ref[...]
    x = x_ref[0].astype(f32)
    x_scale = lax.rsqrt(jnp.mean(x * x, axis=1, keepdims=True) + EPS_NORM)
    x_hat = x * x_scale
    normed = x_hat * gain
    normed_bf = normed.astype(bf16)
    normed_s = (normed_bf, (normed - normed_bf.astype(f32)).astype(bf16))
    proj_ref[...] = dot(normed_bf, win_ref[...])
    bw_s = split(bw_ref[...])
    gate = dot3(normed_s, bw_s)
    gate_sig = sigmoid(gate)
    decay_rate = -jnp.exp(dlog_ref[...])
    softplus = jnp.maximum(gate, 0.0) + jnp.log1p(jnp.exp(-jnp.abs(gate)))
    log_decay = decay_rate * softplus

    row_id = lax.broadcasted_iota(jnp.int32, (length, DK), 0)

    def shifted(value, by):
        if by == 0:
            return value
        rolled = pltpu.roll(value, by % length, axis=0)
        if by > 0:
            return jnp.where(row_id >= by, rolled, 0.0)
        return jnp.where(row_id < length + by, rolled, 0.0)

    def conv_block(at):
        piece = proj_ref[:, at : at + DK]
        acc = None
        for tap in range(CONV):
            term = taps_ref[tap : tap + 1, at : at + DK] * shifted(piece, CONV - 1 - tap)
            acc = term if acc is None else acc + term
        return acc

    for at in range(0, channels, DK):
        conv_ref[:, at : at + DK] = conv_block(at)

    def active(at, wide):
        value = conv_ref[:, at : at + wide]
        return value * sigmoid(value)

    rows = lax.broadcasted_iota(jnp.int32, (chunk, chunk), 0)
    cols = lax.broadcasted_iota(jnp.int32, (chunk, chunk), 1)
    lower_strict = rows > cols
    lower_incl = rows >= cols
    ones_lower = jnp.where(lower_incl, 1.0, 0.0).astype(bf16)
    levels = chunk.bit_length() - 1
    level_masks = [
        ((rows >> level) ^ (cols >> level)) == 1 for level in range(levels)
    ]

    def exact_sum(value, dim):
        high = value.astype(bf16)
        rest = value - high.astype(f32)
        mid = rest.astype(bf16)
        low = (rest - mid.astype(f32)).astype(bf16)
        return (
            dot(ones_lower, low, dim, 0) + dot(ones_lower, mid, dim, 0)
        ) + dot(ones_lower, high, dim, 0)

    cums = [exact_sum(log_decay[c * chunk : (c + 1) * chunk], 1) for c in range(chunks)]
    cums_t = [jnp.transpose(cum) for cum in cums]

    scale = DK ** (-0.5)
    q_hat, q_rs, k_hat, k_rs, vals = ([], [], [], [], [])
    for h in range(H):
        q = active(h * DK, DK)
        k = active((H + h) * DK, DK)
        q_rs.append(lax.rsqrt(row_sum(q * q) + EPS_NORM))
        k_rs.append(lax.rsqrt(row_sum(k * k) + EPS_NORM))
        q_hat.append(q * q_rs[h])
        k_hat.append(k * k_rs[h])
        vals.append(active(2 * H * DK + h * DV, DV))

    units = [(h, c) for h in range(H) for c in range(chunks)]
    info = {}
    for h, c in units:
        span = slice(c * chunk, (c + 1) * chunk)
        k = k_hat[h][span]
        q = q_hat[h][span] * scale
        u = {"k": k, "q": q, "ks": split(k), "qs": split(q), "v": vals[h][span]}
        u["beta"] = gate_sig[span, h : h + 1]
        g = cums[c][:, H + h : H + h + 1]
        g_row = cums_t[c][H + h : H + h + 1, :]
        spread = g - g_row
        u["incl"] = jnp.where(lower_incl, jnp.exp(jnp.where(lower_incl, spread, 0.0)), 0.0)
        u["strict"] = jnp.where(lower_strict, u["incl"], 0.0)
        u["eg"] = jnp.exp(g)
        last = g[chunk - 1 : chunk]
        u["elast"] = jnp.exp(last)
        u["tail"] = jnp.exp(last - g)
        u["a"] = u["beta"] * u["strict"] * dot3(u["ks"], u["ks"], 1, 1)
        u["p"] = split(u["incl"] * dot3(u["qs"], u["ks"], 1, 1))
        info[h, c] = u
    inverses = unit_inverse([info[n]["a"] for n in units], levels, level_masks)
    for n, inverse in zip(units, inverses):
        info[n]["t"] = split(inverse)

    state_out = {}
    for h in range(H):
        state = None
        for c in range(chunks):
            u = info[h, c]
            u["s"] = state
            u["ss"] = None if state is None else split(state)
            if state is None:
                u["e"] = u["v"]
            else:
                u["e"] = u["v"] - u["eg"] * dot3(u["ks"], u["ss"])
            delta = dot3(u["t"], split(u["beta"] * u["e"]))
            u["d"] = split(delta)
            o = dot3(u["p"], u["d"])
            if state is not None:
                o = o + u["eg"] * dot3(u["qs"], u["ss"])
            state_out[h, c] = o
            if c < chunks - 1:
                u["kd"] = split(u["k"] * u["tail"])
                update = dot3(u["kd"], u["d"], 0, 0)
                state = update if state is None else u["elast"] * state + update

    flag = flag_ref[pl.program_id(0)].astype(f32)
    upstream_f = cot_ref[0].astype(f32) * flag
    upstream = upstream_f.astype(bf16)
    ogain = ogain_ref[...]
    o_grads = {}
    d_ogain = None
    for h in range(H):
        o = jnp.concatenate([state_out[h, c] for c in range(chunks)], axis=0)
        o_rs = lax.rsqrt(jnp.mean(o * o, axis=1, keepdims=True) + EPS_NORM)
        o_hat = o * o_rs
        at = channels + h * DV
        z = proj_ref[:, at : at + DV]
        z_sig = sigmoid(z)
        z_act = z * z_sig
        gained = o_hat * ogain
        mixed_ref[:, h * DV : (h + 1) * DV] = (gained * z_act).astype(bf16)
        d_mixed = dot(upstream, wout_ref[h * DV : (h + 1) * DV, :], 1, 1)
        d_z = d_mixed * gained * (z_sig * (1.0 + z * (1.0 - z_sig)))
        dproj_ref[:, at : at + DV] = d_z.astype(bf16)
        d_gained = d_mixed * z_act
        d_ogain = total(d_ogain, col_sum(d_gained * o_hat))
        d_hat = d_gained * ogain
        d_o = o_rs * (d_hat - o_hat * jnp.mean(o_hat * d_hat, axis=1, keepdims=True))
        for c in range(chunks):
            o_grads[h, c] = d_o[c * chunk : (c + 1) * chunk]
    keep(dogain_ref, d_ogain)
    out_ref[0] = x + dot(mixed_ref[...], wout_ref[...])
    keep(gout_ref, dot(mixed_ref[...], upstream, 0, 0))

    d_beta_cols = {}
    d_cum_cols = {}
    for h in range(H):
        d_state = None
        d_q_parts, d_k_parts = ([None] * chunks, [None] * chunks)
        for c in reversed(range(chunks)):
            u = info[h, c]
            span = slice(c * chunk, (c + 1) * chunk)
            d_o = o_grads[h, c]
            d_os = split(d_o)
            d_d = dot3(u["p"], d_os, 0, 0)
            d_qk = split(u["incl"] * dot3(d_os, u["d"], 1, 1))
            d_q = dot3(d_qk, u["ks"])
            d_k_minus = dot3(d_qk, u["qs"], 0, 0)
            d_k_plus = None
            d_last = None
            new_d_state = None
            if d_state is not None:
                d_ss = split(d_state)
                d_kd = u["tail"] * dot3(u["d"], d_ss, 1, 1)
                d_d = d_d + dot3(u["kd"], d_ss)
                d_k_minus = d_k_minus + d_kd
                d_last = jnp.sum(row_sum(u["k"] * d_kd), axis=0, keepdims=True)
                if u["s"] is not None:
                    d_last = d_last + u["elast"] * jnp.sum(
                        row_sum(u["s"] * d_state), axis=0, keepdims=True
                    )
                    new_d_state = u["elast"] * d_state
            d_r = dot3(u["t"], split(d_d), 0, 0)
            d_rs = split(d_r)
            hold = split(-u["strict"] * dot3(d_rs, u["d"], 1, 1))
            hold_k = dot3(hold, u["ks"])
            d_beta = row_sum(d_r * u["e"]) + row_sum(u["k"] * hold_k)
            d_k_plus = u["beta"] * hold_k
            d_k_minus = d_k_minus + dot3(hold, split(u["beta"] * u["k"]), 0, 0)
            d_e = u["beta"] * d_r
            dact_ref[span, 2 * H * DK + h * DV : 2 * H * DK + (h + 1) * DV] = d_e
            if u["s"] is not None:
                d_os_g = split(u["eg"] * d_o)
                d_es_g = split(-u["eg"] * d_e)
                d_q = d_q + dot3(d_os_g, u["ss"], 1, 1)
                d_k_plus = d_k_plus + dot3(d_es_g, u["ss"], 1, 1)
                new_d_state = total(
                    new_d_state,
                    dot3(u["qs"], d_os_g, 0, 0),
                    dot3(u["ks"], d_es_g, 0, 0),
                )
            d_cum = row_sum(u["q"] * d_q + u["k"] * (d_k_plus - d_k_minus))
            if d_last is not None:
                tail_row = lax.broadcasted_iota(jnp.int32, (chunk, 1), 0) == chunk - 1
                d_cum = d_cum + jnp.where(tail_row, d_last, 0.0)
            d_beta_cols[h, c] = d_beta
            d_cum_cols[h, c] = d_cum
            d_q_parts[c] = d_q
            d_k_parts[c] = d_k_plus + d_k_minus
            d_state = new_d_state
        d_q = jnp.concatenate(d_q_parts, axis=0) * scale
        d_k = jnp.concatenate(d_k_parts, axis=0)
        dact_ref[:, h * DK : (h + 1) * DK] = q_rs[h] * (
            d_q - q_hat[h] * row_sum(q_hat[h] * d_q)
        )
        dact_ref[:, (H + h) * DK : (H + h + 1) * DK] = k_rs[h] * (
            d_k - k_hat[h] * row_sum(k_hat[h] * d_k)
        )

    lane = lax.broadcasted_iota(jnp.int32, (chunk, lanes), 1)
    d_gate_parts = []
    d_dlog = None
    for c in range(chunks):
        span = slice(c * chunk, (c + 1) * chunk)
        d_cum = jnp.zeros((chunk, lanes), f32)
        d_beta = jnp.zeros((chunk, lanes), f32)
        for h in range(H):
            d_cum = jnp.where(lane == H + h, d_cum_cols[h, c], d_cum)
            d_beta = jnp.where(lane == h, d_beta_cols[h, c], d_beta)
        d_log = exact_sum(d_cum, 0)
        d_dlog = total(d_dlog, col_sum(d_log * log_decay[span]))
        sig = gate_sig[span]
        d_gate_parts.append(d_beta * sig * (1.0 - sig) + d_log * decay_rate * sig)
    keep(ddlog_ref, d_dlog)
    d_gate = jnp.concatenate(d_gate_parts, axis=0)
    d_gate_s = split(d_gate)
    keep(dbw_ref, dot3(normed_s, d_gate_s, 0, 0))

    d_taps = []
    for at in range(0, channels, DK):
        conv = conv_ref[:, at : at + DK]
        sig = sigmoid(conv)
        d_conv = dact_ref[:, at : at + DK] * (sig * (1.0 + conv * (1.0 - sig)))
        piece = proj_ref[:, at : at + DK]
        d_piece = None
        tap_rows = []
        for tap in range(CONV):
            by = CONV - 1 - tap
            tap_rows.append(col_sum(d_conv * shifted(piece, by)))
            d_piece = total(
                d_piece, taps_ref[tap : tap + 1, at : at + DK] * shifted(d_conv, -by)
            )
        dproj_ref[:, at : at + DK] = d_piece.astype(bf16)
        d_taps.append(jnp.concatenate(tap_rows, axis=0))
    keep(dtaps_ref, jnp.concatenate(d_taps, axis=1))

    keep(gin_ref, dot(normed_bf, dproj_ref[...], 0, 0))
    d_normed = dot(dproj_ref[...], win_ref[...], 1, 1) + dot3(d_gate_s, bw_s, 1, 1)
    keep(dgain_ref, col_sum(d_normed * x_hat))
    d_hat = d_normed * gain
    d_x = x_scale * (d_hat - x_hat * jnp.mean(x_hat * d_hat, axis=1, keepdims=True))
    xgrad_ref[0] = upstream.astype(f32) + d_x


def local_step(
    seq_valid, block_input, cotangent, in_full, out_full, gain, bw, taps, dlog, ogain
):
    seqs, length, width = block_input.shape
    proj_cols = in_full.shape[1]
    mixed_cols = out_full.shape[0]
    channels = taps.shape[1]
    f32 = jnp.float32
    token = pl.BlockSpec((1, length, width), lambda i: (i, 0, 0))

    def whole(shape):
        return pl.BlockSpec(shape, lambda i: (0, 0))

    sums = [
        in_full.shape,
        out_full.shape,
        gain.shape,
        bw.shape,
        taps.shape,
        dlog.shape,
        ogain.shape,
    ]
    return pl.pallas_call(
        functools.partial(local_kernel, seqs=seqs),
        grid=(seqs,),
        in_specs=[pl.BlockSpec(memory_space=pltpu.SMEM), token, token]
        + [whole(shape) for shape in sums],
        out_specs=[token, token] + [whole(shape) for shape in sums],
        out_shape=[jax.ShapeDtypeStruct(block_input.shape, f32)] * 2
        + [jax.ShapeDtypeStruct(shape, f32) for shape in sums],
        scratch_shapes=[
            pltpu.VMEM((length, proj_cols), f32),
            pltpu.VMEM((length, channels), f32),
            pltpu.VMEM((length, mixed_cols), jnp.bfloat16),
            pltpu.VMEM((length, proj_cols), jnp.bfloat16),
            pltpu.VMEM((length, channels), f32),
        ],
        compiler_params=pltpu.CompilerParams(
            dimension_semantics=("arbitrary",), vmem_limit_bytes=60 * 1024 * 1024
        ),
        name="local_step",
    )(seq_valid, block_input, cotangent, in_full, out_full, gain, bw, taps, dlog, ogain)


def adamw(weight, grad, moment, second):
    moment_new = BETA_ONE * moment + (1.0 - BETA_ONE) * grad
    second_new = BETA_TWO * second + (1.0 - BETA_TWO) * grad * grad
    update = (
        moment_new
        / (1.0 - BETA_ONE**STEP)
        / (jnp.sqrt(second_new / (1.0 - BETA_TWO**STEP)) + ADAM_EPS)
    )
    return (weight - LEARN_RATE * (update + WEIGHT_DECAY * weight), moment_new, second_new)


def on_device(
    block_input,
    cotangent,
    seq_valid,
    in_weight,
    out_weight,
    small_params,
    in_moment,
    in_second,
    out_moment,
    out_second,
    small_moment,
    small_second,
):
    gain_in, beta_weight, conv_taps, decay_log, out_gain = split_small(small_params)
    in_full = lax.all_gather(in_weight.astype(jnp.bfloat16), "fsdp", axis=0, tiled=True)
    out_full = lax.all_gather(out_weight.astype(jnp.bfloat16), "fsdp", axis=0, tiled=True)
    lanes = 128
    (
        block_output,
        input_grad,
        in_local,
        out_local,
        d_gain_in,
        d_beta_weight,
        d_conv,
        d_decay,
        d_gain_out,
    ) = local_step(
        seq_valid,
        block_input,
        cotangent,
        in_full,
        out_full,
        gain_in[None],
        jnp.pad(beta_weight, ((0, 0), (0, lanes - 2 * H))),
        conv_taps,
        jnp.pad(decay_log[None], ((0, 0), (H, lanes - 2 * H))),
        out_gain[None],
    )
    in_owned = lax.psum_scatter(
        in_local, "fsdp", scatter_dimension=0, tiled=True
    )
    out_owned = lax.psum_scatter(
        out_local, "fsdp", scatter_dimension=0, tiled=True
    )
    in_grad, out_grad = lax.psum((in_owned, out_owned), "rep")
    small_local = jnp.concatenate(
        [
            d_gain_in[0],
            d_beta_weight[:, : 2 * H].reshape(-1),
            d_conv.reshape(-1),
            d_decay[0, H : 2 * H],
            d_gain_out[0],
        ]
    )
    small_grad = lax.psum(small_local, ("rep", "fsdp"))
    new_in, in_m, in_v = adamw(in_weight, in_grad, in_moment, in_second)
    new_out, out_m, out_v = adamw(out_weight, out_grad, out_moment, out_second)
    new_small, small_m, small_v = adamw(small_params, small_grad, small_moment, small_second)
    return (
        block_output,
        input_grad,
        in_grad,
        out_grad,
        small_grad,
        new_in,
        new_out,
        new_small,
        in_m,
        in_v,
        out_m,
        out_v,
        small_m,
        small_v,
    )


def solution(mesh):
    in_specs = (
        P(("rep", "fsdp"), None, None),
        P(("rep", "fsdp"), None, None),
        P(("rep", "fsdp")),
        P("fsdp", None),
        P("fsdp", None),
        P(),
        P("fsdp", None),
        P("fsdp", None),
        P("fsdp", None),
        P("fsdp", None),
        P(),
        P(),
    )
    out_specs = (
        P(("rep", "fsdp"), None, None),
        P(("rep", "fsdp"), None, None),
        P("fsdp", None),
        P("fsdp", None),
        P(),
        P("fsdp", None),
        P("fsdp", None),
        P(),
        P("fsdp", None),
        P("fsdp", None),
        P("fsdp", None),
        P("fsdp", None),
        P(),
        P(),
    )
    return jax.shard_map(
        on_device, mesh=mesh, in_specs=in_specs, out_specs=out_specs, check_vma=False
    )
```

```python
import functools

import jax
import jax.numpy as jnp
from jax import lax
from jax.experimental import pallas as pl
from jax.experimental.pallas import tpu as pltpu
from jax.sharding import PartitionSpec as P

D = 512
H = 2
DK = 128
DV = 256
CONV = 4
CHUNK = 128
GROUPS = 4
MESH = pl.DeviceIdType.MESH
STEP = 3


EPS_NORM = 1e-06
BETA_ONE = 0.9
BETA_TWO = 0.95
ADAM_EPS = 1e-08
LEARN_RATE = 0.01
WEIGHT_DECAY = 0.1


def split_small(small):
    channels = 2 * H * DK + H * DV
    first = D
    second = first + D * 2 * H
    third = second + CONV * channels
    fourth = third + H
    return (
        small[:first],
        small[first:second].reshape(D, 2 * H),
        small[second:third].reshape(CONV, channels),
        small[third:fourth],
        small[fourth:],
    )


def split(value):
    high = value.astype(jnp.bfloat16)
    return (high, (value - high.astype(jnp.float32)).astype(jnp.bfloat16))


def dot(left, right, left_dim=1, right_dim=0):
    return lax.dot_general(
        left,
        right,
        (((left_dim,), (right_dim,)), ((), ())),
        preferred_element_type=jnp.float32,
    )


def dot3(left, right, left_dim=1, right_dim=0):
    return (
        dot(left[0], right[1], left_dim, right_dim)
        + dot(left[1], right[0], left_dim, right_dim)
    ) + dot(left[0], right[0], left_dim, right_dim)


def row_sum(value):
    return jnp.sum(value, axis=1, keepdims=True)


def col_sum(value):
    return jnp.sum(value, axis=0, keepdims=True)


def sigmoid(value):
    return 1.0 / (1.0 + jnp.exp(-value))


def total(*terms):
    out = None
    for term in terms:
        if term is not None:
            out = term if out is None else out + term
    return out


def unit_inverse(strict, levels, level_masks):
    size = strict[0].shape[0]
    rows = lax.broadcasted_iota(jnp.int32, (size, size), 0)
    cols = lax.broadcasted_iota(jnp.int32, (size, size), 1)
    eye = jnp.where(rows == cols, 1.0, 0.0)
    inverses = [eye - jnp.where(level_masks[0], a, 0.0) for a in strict]
    for level in range(1, levels):
        for n, a in enumerate(strict):
            inv = split(inverses[n])
            inner = dot3(inv, split(jnp.where(level_masks[level], a, 0.0)))
            inverses[n] = inverses[n] - dot3(split(inner), inv)
    return inverses


def local_kernel(
    flag_ref,
    x_ref,
    cot_ref,
    blocks_ref,
    gain_ref,
    bw_ref,
    taps_ref,
    dlog_ref,
    ogain_ref,
    out_ref,
    xgrad_ref,
    grad_ref,
    dgain_ref,
    dbw_ref,
    dtaps_ref,
    ddlog_ref,
    dogain_ref,
    proj_ref,
    conv_ref,
    mixed_ref,
    dproj_ref,
    dact_ref,
    win_ref,
    wout_ref,
    *,
    seqs,
):
    f32, bf16 = jnp.float32, jnp.bfloat16
    length, width = x_ref.shape[1:]
    channels = taps_ref.shape[1]
    lanes = bw_ref.shape[1]
    chunk = CHUNK if length % CHUNK == 0 else length
    chunks = length // chunk

    def keep(ref, value):
        if seqs == 1:
            ref[...] = value
        else:

            @pl.when(pl.program_id(0) == 0)
            def _():
                ref[...] = value

            @pl.when(pl.program_id(0) > 0)
            def _():
                ref[...] = ref[...] + value

    shards, col_blocks, shard_rows, block = blocks_ref.shape
    in_blocks = win_ref.shape[1] // block
    out_blocks = wout_ref.shape[1] // block
    for s in range(shards):
        here = slice(s * shard_rows, (s + 1) * shard_rows)
        for b in range(in_blocks):
            win_ref[here, b * block : (b + 1) * block] = blocks_ref[s, b]
        for b in range(out_blocks):
            wout_ref[here, b * block : (b + 1) * block] = blocks_ref[s, in_blocks + b]

    def keep_blocks(value, first):
        for s in range(shards):
            here = slice(s * shard_rows, (s + 1) * shard_rows)
            for b in range(value.shape[1] // block):
                keep(grad_ref.at[s, first + b], value[here, b * block : (b + 1) * block])

    gain = gain_ref[...]
    x = x_ref[0].astype(f32)
    x_scale = lax.rsqrt(jnp.mean(x * x, axis=1, keepdims=True) + EPS_NORM)
    x_hat = x * x_scale
    normed = x_hat * gain
    normed_bf = normed.astype(bf16)
    normed_s = (normed_bf, (normed - normed_bf.astype(f32)).astype(bf16))
    proj_ref[...] = dot(normed_bf, win_ref[...])
    bw_s = split(bw_ref[...])
    gate = dot3(normed_s, bw_s)
    gate_sig = sigmoid(gate)
    decay_rate = -jnp.exp(dlog_ref[...])
    softplus = jnp.maximum(gate, 0.0) + jnp.log1p(jnp.exp(-jnp.abs(gate)))
    log_decay = decay_rate * softplus

    row_id = lax.broadcasted_iota(jnp.int32, (length, DK), 0)

    def shifted(value, by):
        if by == 0:
            return value
        rolled = pltpu.roll(value, by % length, axis=0)
        if by > 0:
            return jnp.where(row_id >= by, rolled, 0.0)
        return jnp.where(row_id < length + by, rolled, 0.0)

    def conv_block(at):
        piece = proj_ref[:, at : at + DK]
        acc = None
        for tap in range(CONV):
            term = taps_ref[tap : tap + 1, at : at + DK] * shifted(piece, CONV - 1 - tap)
            acc = term if acc is None else acc + term
        return acc

    for at in range(0, channels, DK):
        conv_ref[:, at : at + DK] = conv_block(at)

    def active(at, wide):
        value = conv_ref[:, at : at + wide]
        return value * sigmoid(value)

    rows = lax.broadcasted_iota(jnp.int32, (chunk, chunk), 0)
    cols = lax.broadcasted_iota(jnp.int32, (chunk, chunk), 1)
    lower_strict = rows > cols
    lower_incl = rows >= cols
    ones_lower = jnp.where(lower_incl, 1.0, 0.0).astype(bf16)
    levels = chunk.bit_length() - 1
    level_masks = [
        ((rows >> level) ^ (cols >> level)) == 1 for level in range(levels)
    ]

    def exact_sum(value, dim):
        high = value.astype(bf16)
        rest = value - high.astype(f32)
        mid = rest.astype(bf16)
        low = (rest - mid.astype(f32)).astype(bf16)
        return (
            dot(ones_lower, low, dim, 0) + dot(ones_lower, mid, dim, 0)
        ) + dot(ones_lower, high, dim, 0)

    cums = [exact_sum(log_decay[c * chunk : (c + 1) * chunk], 1) for c in range(chunks)]
    cums_t = [jnp.transpose(cum) for cum in cums]

    scale = DK ** (-0.5)
    q_hat, q_rs, k_hat, k_rs, vals = ([], [], [], [], [])
    for h in range(H):
        q = active(h * DK, DK)
        k = active((H + h) * DK, DK)
        q_rs.append(lax.rsqrt(row_sum(q * q) + EPS_NORM))
        k_rs.append(lax.rsqrt(row_sum(k * k) + EPS_NORM))
        q_hat.append(q * q_rs[h])
        k_hat.append(k * k_rs[h])
        vals.append(active(2 * H * DK + h * DV, DV))

    units = [(h, c) for h in range(H) for c in range(chunks)]
    info = {}
    for h, c in units:
        span = slice(c * chunk, (c + 1) * chunk)
        k = k_hat[h][span]
        q = q_hat[h][span] * scale
        u = {"k": k, "q": q, "ks": split(k), "qs": split(q), "v": vals[h][span]}
        u["beta"] = gate_sig[span, h : h + 1]
        g = cums[c][:, H + h : H + h + 1]
        g_row = cums_t[c][H + h : H + h + 1, :]
        spread = g - g_row
        u["incl"] = jnp.where(lower_incl, jnp.exp(jnp.where(lower_incl, spread, 0.0)), 0.0)
        u["strict"] = jnp.where(lower_strict, u["incl"], 0.0)
        u["eg"] = jnp.exp(g)
        last = g[chunk - 1 : chunk]
        u["elast"] = jnp.exp(last)
        u["tail"] = jnp.exp(last - g)
        u["a"] = u["beta"] * u["strict"] * dot3(u["ks"], u["ks"], 1, 1)
        u["p"] = split(u["incl"] * dot3(u["qs"], u["ks"], 1, 1))
        info[h, c] = u
    inverses = unit_inverse([info[n]["a"] for n in units], levels, level_masks)
    for n, inverse in zip(units, inverses):
        info[n]["t"] = split(inverse)

    state_out = {}
    for h in range(H):
        state = None
        for c in range(chunks):
            u = info[h, c]
            u["s"] = state
            u["ss"] = None if state is None else split(state)
            if state is None:
                u["e"] = u["v"]
            else:
                u["e"] = u["v"] - u["eg"] * dot3(u["ks"], u["ss"])
            delta = dot3(u["t"], split(u["beta"] * u["e"]))
            u["d"] = split(delta)
            o = dot3(u["p"], u["d"])
            if state is not None:
                o = o + u["eg"] * dot3(u["qs"], u["ss"])
            state_out[h, c] = o
            if c < chunks - 1:
                u["kd"] = split(u["k"] * u["tail"])
                update = dot3(u["kd"], u["d"], 0, 0)
                state = update if state is None else u["elast"] * state + update

    flag = flag_ref[pl.program_id(0)].astype(f32)
    upstream_f = cot_ref[0].astype(f32) * flag
    upstream = upstream_f.astype(bf16)
    ogain = ogain_ref[...]
    o_grads = {}
    d_ogain = None
    for h in range(H):
        o = jnp.concatenate([state_out[h, c] for c in range(chunks)], axis=0)
        o_rs = lax.rsqrt(jnp.mean(o * o, axis=1, keepdims=True) + EPS_NORM)
        o_hat = o * o_rs
        at = channels + h * DV
        z = proj_ref[:, at : at + DV]
        z_sig = sigmoid(z)
        z_act = z * z_sig
        gained = o_hat * ogain
        mixed_ref[:, h * DV : (h + 1) * DV] = (gained * z_act).astype(bf16)
        d_mixed = dot(upstream, wout_ref[h * DV : (h + 1) * DV, :], 1, 1)
        d_z = d_mixed * gained * (z_sig * (1.0 + z * (1.0 - z_sig)))
        dproj_ref[:, at : at + DV] = d_z.astype(bf16)
        d_gained = d_mixed * z_act
        d_ogain = total(d_ogain, col_sum(d_gained * o_hat))
        d_hat = d_gained * ogain
        d_o = o_rs * (d_hat - o_hat * jnp.mean(o_hat * d_hat, axis=1, keepdims=True))
        for c in range(chunks):
            o_grads[h, c] = d_o[c * chunk : (c + 1) * chunk]
    keep(dogain_ref, d_ogain)
    out_ref[0] = x + dot(mixed_ref[...], wout_ref[...])
    keep_blocks(dot(mixed_ref[...], upstream, 0, 0), in_blocks)

    d_beta_cols = {}
    d_cum_cols = {}
    for h in range(H):
        d_state = None
        d_q_parts, d_k_parts = ([None] * chunks, [None] * chunks)
        for c in reversed(range(chunks)):
            u = info[h, c]
            span = slice(c * chunk, (c + 1) * chunk)
            d_o = o_grads[h, c]
            d_os = split(d_o)
            d_d = dot3(u["p"], d_os, 0, 0)
            d_qk = split(u["incl"] * dot3(d_os, u["d"], 1, 1))
            d_q = dot3(d_qk, u["ks"])
            d_k_minus = dot3(d_qk, u["qs"], 0, 0)
            d_k_plus = None
            d_last = None
            new_d_state = None
            if d_state is not None:
                d_ss = split(d_state)
                d_kd = u["tail"] * dot3(u["d"], d_ss, 1, 1)
                d_d = d_d + dot3(u["kd"], d_ss)
                d_k_minus = d_k_minus + d_kd
                d_last = jnp.sum(row_sum(u["k"] * d_kd), axis=0, keepdims=True)
                if u["s"] is not None:
                    d_last = d_last + u["elast"] * jnp.sum(
                        row_sum(u["s"] * d_state), axis=0, keepdims=True
                    )
                    new_d_state = u["elast"] * d_state
            d_r = dot3(u["t"], split(d_d), 0, 0)
            d_rs = split(d_r)
            hold = split(-u["strict"] * dot3(d_rs, u["d"], 1, 1))
            hold_k = dot3(hold, u["ks"])
            d_beta = row_sum(d_r * u["e"]) + row_sum(u["k"] * hold_k)
            d_k_plus = u["beta"] * hold_k
            d_k_minus = d_k_minus + dot3(hold, split(u["beta"] * u["k"]), 0, 0)
            d_e = u["beta"] * d_r
            dact_ref[span, 2 * H * DK + h * DV : 2 * H * DK + (h + 1) * DV] = d_e
            if u["s"] is not None:
                d_os_g = split(u["eg"] * d_o)
                d_es_g = split(-u["eg"] * d_e)
                d_q = d_q + dot3(d_os_g, u["ss"], 1, 1)
                d_k_plus = d_k_plus + dot3(d_es_g, u["ss"], 1, 1)
                new_d_state = total(
                    new_d_state,
                    dot3(u["qs"], d_os_g, 0, 0),
                    dot3(u["ks"], d_es_g, 0, 0),
                )
            d_cum = row_sum(u["q"] * d_q + u["k"] * (d_k_plus - d_k_minus))
            if d_last is not None:
                tail_row = lax.broadcasted_iota(jnp.int32, (chunk, 1), 0) == chunk - 1
                d_cum = d_cum + jnp.where(tail_row, d_last, 0.0)
            d_beta_cols[h, c] = d_beta
            d_cum_cols[h, c] = d_cum
            d_q_parts[c] = d_q
            d_k_parts[c] = d_k_plus + d_k_minus
            d_state = new_d_state
        d_q = jnp.concatenate(d_q_parts, axis=0) * scale
        d_k = jnp.concatenate(d_k_parts, axis=0)
        dact_ref[:, h * DK : (h + 1) * DK] = q_rs[h] * (
            d_q - q_hat[h] * row_sum(q_hat[h] * d_q)
        )
        dact_ref[:, (H + h) * DK : (H + h + 1) * DK] = k_rs[h] * (
            d_k - k_hat[h] * row_sum(k_hat[h] * d_k)
        )

    lane = lax.broadcasted_iota(jnp.int32, (chunk, lanes), 1)
    d_gate_parts = []
    d_dlog = None
    for c in range(chunks):
        span = slice(c * chunk, (c + 1) * chunk)
        d_cum = jnp.zeros((chunk, lanes), f32)
        d_beta = jnp.zeros((chunk, lanes), f32)
        for h in range(H):
            d_cum = jnp.where(lane == H + h, d_cum_cols[h, c], d_cum)
            d_beta = jnp.where(lane == h, d_beta_cols[h, c], d_beta)
        d_log = exact_sum(d_cum, 0)
        d_dlog = total(d_dlog, col_sum(d_log * log_decay[span]))
        sig = gate_sig[span]
        d_gate_parts.append(d_beta * sig * (1.0 - sig) + d_log * decay_rate * sig)
    keep(ddlog_ref, d_dlog)
    d_gate = jnp.concatenate(d_gate_parts, axis=0)
    d_gate_s = split(d_gate)
    keep(dbw_ref, dot3(normed_s, d_gate_s, 0, 0))

    d_taps = []
    for at in range(0, channels, DK):
        conv = conv_ref[:, at : at + DK]
        sig = sigmoid(conv)
        d_conv = dact_ref[:, at : at + DK] * (sig * (1.0 + conv * (1.0 - sig)))
        piece = proj_ref[:, at : at + DK]
        d_piece = None
        tap_rows = []
        for tap in range(CONV):
            by = CONV - 1 - tap
            tap_rows.append(col_sum(d_conv * shifted(piece, by)))
            d_piece = total(
                d_piece, taps_ref[tap : tap + 1, at : at + DK] * shifted(d_conv, -by)
            )
        dproj_ref[:, at : at + DK] = d_piece.astype(bf16)
        d_taps.append(jnp.concatenate(tap_rows, axis=0))
    keep(dtaps_ref, jnp.concatenate(d_taps, axis=1))

    keep_blocks(dot(normed_bf, dproj_ref[...], 0, 0), 0)
    d_normed = dot(dproj_ref[...], win_ref[...], 1, 1) + dot3(d_gate_s, bw_s, 1, 1)
    keep(dgain_ref, col_sum(d_normed * x_hat))
    d_hat = d_normed * gain
    d_x = x_scale * (d_hat - x_hat * jnp.mean(x_hat * d_hat, axis=1, keepdims=True))
    xgrad_ref[0] = upstream.astype(f32) + d_x


def local_step(
    seq_valid, block_input, cotangent, blocks, gain, bw, taps, dlog, ogain, in_cols
):
    seqs, length, width = block_input.shape
    shards, col_blocks, shard_rows, block = blocks.shape
    out_cols = col_blocks * block - in_cols
    channels = taps.shape[1]
    f32 = jnp.float32
    token = pl.BlockSpec((1, length, width), lambda i: (i, 0, 0))

    def whole(shape):
        return pl.BlockSpec(shape, lambda i: (0,) * len(shape))

    sums = [blocks.shape, gain.shape, bw.shape, taps.shape, dlog.shape, ogain.shape]
    return pl.pallas_call(
        functools.partial(local_kernel, seqs=seqs),
        grid=(seqs,),
        in_specs=[pl.BlockSpec(memory_space=pltpu.SMEM), token, token]
        + [whole(shape) for shape in sums],
        out_specs=[token, token] + [whole(shape) for shape in sums],
        out_shape=[jax.ShapeDtypeStruct(block_input.shape, f32)] * 2
        + [jax.ShapeDtypeStruct(shape, f32) for shape in sums],
        scratch_shapes=[
            pltpu.VMEM((length, in_cols), f32),
            pltpu.VMEM((length, channels), f32),
            pltpu.VMEM((length, H * DV), jnp.bfloat16),
            pltpu.VMEM((length, in_cols), jnp.bfloat16),
            pltpu.VMEM((length, channels), f32),
            pltpu.VMEM((shards * shard_rows, in_cols), jnp.bfloat16),
            pltpu.VMEM((shards * shard_rows, out_cols), jnp.bfloat16),
        ],
        compiler_params=pltpu.CompilerParams(
            dimension_semantics=("arbitrary",), vmem_limit_bytes=60 * 1024 * 1024
        ),
        name="local_step",
    )(seq_valid, block_input, cotangent, blocks, gain, bw, taps, dlog, ogain)


def greet(replicas, shards):
    rep, shard = lax.axis_index("rep"), lax.axis_index("fsdp")
    barrier = pltpu.get_barrier_semaphore()
    bits = replicas.bit_length() - 1
    for bit in range(bits):
        pl.semaphore_signal(
            barrier, inc=1, device_id=(flip(rep, bit), shard), device_id_type=MESH
        )
    for step in range(1, shards):
        pl.semaphore_signal(
            barrier,
            inc=1,
            device_id=(rep, lax.rem(shard + step, shards)),
            device_id_type=MESH,
        )
    pl.semaphore_wait(barrier, bits + shards - 1)


def bit_of(rep, bit):
    return lax.rem(rep // (1 << bit), 2)


def flip(rep, bit):
    return rep + (1 << bit) * (1 - 2 * bit_of(rep, bit))


def bit_orders(replicas):
    bits = list(range(replicas.bit_length() - 1))
    return [bits, bits[:1] + bits[1:][::-1]]


def aligned(offset, size):
    return pl.ds(pl.multiple_of(offset, size), size)


class Copies:
    def __init__(self, send_sems, recv_sems):
        self.send_sems, self.recv_sems, self.started = send_sems, recv_sems, []

    def start(self, src, dst, rep, shard):
        at = len(self.started)
        copy = pltpu.make_async_remote_copy(
            src_ref=src,
            dst_ref=dst,
            send_sem=self.send_sems.at[at],
            recv_sem=self.recv_sems.at[at],
            device_id=(rep, shard),
            device_id_type=MESH,
        )
        copy.start()
        self.started.append(copy)
        return copy

    def finish(self):
        for copy in self.started:
            copy.wait_send()


def gather_kernel(replicas, shards, win_ref, wout_ref, full_ref, mine_ref, send_sems, recv_sems):
    rep, shard = lax.axis_index("rep"), lax.axis_index("fsdp")
    rows, block = win_ref.shape[0], full_ref.shape[-1]
    at = 0
    for ref in (win_ref, wout_ref):
        for b in range(ref.shape[1] // block):
            value = ref[:, b * block : (b + 1) * block].astype(jnp.bfloat16)
            mine_ref[at : at + rows, :] = value
            at += rows
    full_ref[shard] = mine_ref[...]
    greet(replicas, shards)
    copies = Copies(send_sems, recv_sems)
    orders = bit_orders(replicas)
    span = mine_ref.shape[0] // len(orders)
    state = []
    for g, order in enumerate(orders):
        size, base = span, g * span
        for bit in order:
            size //= 2
            base = base + bit_of(rep, bit) * size
        pending = []
        for step in range(1, shards):
            pending.append(
                copies.start(
                    mine_ref.at[aligned(base, size), :],
                    full_ref.at[shard, aligned(base, size), :],
                    rep,
                    lax.rem(shard + step, shards),
                )
            )
        state.append([base, size, pending])
    for level in range(len(orders[0])):
        for g, order in enumerate(orders):
            base, size, pending = state[g]
            for copy in pending:
                copy.wait_recv()
            bit = order[len(order) - 1 - level]
            here = full_ref.at[:, aligned(base, size), :]
            pending = [copies.start(here, here, flip(rep, bit), shard)]
            state[g] = [base - bit_of(rep, bit) * size, 2 * size, pending]
    for _, _, pending in state:
        for copy in pending:
            copy.wait_recv()
    copies.finish()


def gather_weights(replicas, shards, in_weight, out_weight):
    rows, block = in_weight.shape[0], 128
    total_rows = rows * (in_weight.shape[1] + out_weight.shape[1]) // block
    bits = replicas.bit_length() - 1
    count = 2 * (bits + shards - 1)
    return pl.pallas_call(
        functools.partial(gather_kernel, replicas, shards),
        in_specs=[pl.BlockSpec(memory_space=pltpu.VMEM)] * 2,
        out_specs=pl.BlockSpec(memory_space=pltpu.VMEM),
        out_shape=jax.ShapeDtypeStruct((shards, total_rows, block), jnp.bfloat16),
        scratch_shapes=[
            pltpu.VMEM((total_rows, block), jnp.bfloat16),
            pltpu.SemaphoreType.DMA((count,)),
            pltpu.SemaphoreType.DMA((count,)),
        ],
        compiler_params=pltpu.CompilerParams(
            collective_id=0, has_side_effects=True, vmem_limit_bytes=24 * 1024 * 1024
        ),
        name="gather_weights",
    )(in_weight, out_weight)


def reduce_kernel(replicas, shards, grad_ref, small_ref, out_ref, small_out_ref, *scratch):
    rep, shard = lax.axis_index("rep"), lax.axis_index("fsdp")
    send_sems, recv_sems = scratch[-2:]
    orders = bit_orders(replicas)
    bits = len(orders[0])
    copies = Copies(send_sems, recv_sems)
    greet(replicas, shards)
    span = grad_ref.shape[1] // GROUPS
    groups = []
    for g in range(GROUPS + 1):
        bufs = scratch[g * (bits + 1) : (g + 1) * (bits + 1)]
        if g < GROUPS:
            groups.append([grad_ref, out_ref, g * span, span, orders[g % 2], bufs])
        else:
            groups.append(
                [small_ref, small_out_ref, 0, small_ref.shape[1], orders[0], bufs]
            )

    def halve(group, level):
        cur, _, base, size, order, bufs = group
        half = size // 2
        mine = bit_of(rep, order[level])
        there = base + (1 - mine) * half
        copy = copies.start(
            cur.at[:, aligned(there, half), :], bufs[level], flip(rep, order[level]), shard
        )
        return copy, base + mine * half, half

    live = [halve(group, 0) for group in groups]
    for level in range(bits):
        for g, group in enumerate(groups):
            copy, mine, half = live[g]
            cur, bufs = group[0], group[5]
            copy.wait_recv()
            bufs[level][...] = bufs[level][...] + cur[:, aligned(mine, half), :]
            group[0], group[2], group[3] = bufs[level], 0, half
            if level + 1 < bits:
                live[g] = halve(group, level + 1)
            else:
                pending = []
                for step in range(1, shards):
                    to = lax.rem(shard + step, shards)
                    if g < GROUPS:
                        src, slot = group[0].at[to], bufs[bits].at[step - 1]
                    else:
                        src, slot = group[0].at[0], bufs[bits].at[shard]
                    pending.append(copies.start(src, slot, rep, to))
                live[g] = pending
    spread = []
    for g, group in enumerate(groups):
        cur, out, _, size, order, bufs = group
        base = g * span if g < GROUPS else 0
        full = span if g < GROUPS else small_ref.shape[1]
        for bit in order:
            full //= 2
            base = base + bit_of(rep, bit) * full
        if g == GROUPS:
            bufs[bits][shard] = cur[0]
        for copy in live[g]:
            copy.wait_recv()
        if g < GROUPS:
            value = cur[shard]
            for step in range(1, shards):
                value = value + bufs[bits][step - 1]
        else:
            value = bufs[bits][0]
            for s in range(1, shards):
                value = value + bufs[bits][s]
        out[aligned(base, size), :] = value
        spread.append([base, size, None])
        start_spread(copies, out, spread[g], order[-1], rep, shard)
    for level in range(1, bits + 1):
        for g, group in enumerate(groups):
            spread[g][2].wait_recv()
            if level < bits:
                start_spread(
                    copies, group[1], spread[g], group[4][bits - 1 - level], rep, shard
                )
    copies.finish()


def start_spread(copies, out, state, bit, rep, shard):
    base, size, _ = state
    here = out.at[aligned(base, size), :]
    copy = copies.start(here, here, flip(rep, bit), shard)
    state[:] = [base - bit_of(rep, bit) * size, 2 * size, copy]


def reduce_grads(replicas, shards, grads, small):
    rows, block = grads.shape[1:]
    bits = replicas.bit_length() - 1
    scratch = []
    for g in range(GROUPS + 1):
        parts, size = (shards, rows // GROUPS) if g < GROUPS else (1, small.shape[1])
        for _ in range(bits):
            size //= 2
            scratch.append(pltpu.VMEM((parts, size, block), jnp.float32))
        slots = shards - 1 if g < GROUPS else shards
        scratch.append(pltpu.VMEM((slots, size, block), jnp.float32))
    count = (GROUPS + 1) * (2 * bits + shards - 1)
    return pl.pallas_call(
        functools.partial(reduce_kernel, replicas, shards),
        in_specs=[pl.BlockSpec(memory_space=pltpu.VMEM)] * 2,
        out_specs=[pl.BlockSpec(memory_space=pltpu.VMEM)] * 2,
        out_shape=[
            jax.ShapeDtypeStruct((rows, block), jnp.float32),
            jax.ShapeDtypeStruct(small.shape[1:], jnp.float32),
        ],
        scratch_shapes=scratch
        + [pltpu.SemaphoreType.DMA((count,)), pltpu.SemaphoreType.DMA((count,))],
        compiler_params=pltpu.CompilerParams(
            collective_id=1, has_side_effects=True, vmem_limit_bytes=40 * 1024 * 1024
        ),
        name="reduce_grads",
    )(grads, small)


def adam_kernel(grad_ref, *refs):
    rows, block = refs[0].shape[0], grad_ref.shape[1]
    at = 0
    for first in (0, 3):
        weight, moment, second = refs[first : first + 3]
        outs = refs[6 + 4 * (first // 3) : 10 + 4 * (first // 3)]
        for b in range(weight.shape[1] // block):
            cols = slice(b * block, (b + 1) * block)
            grad = grad_ref[at : at + rows, :]
            at += rows
            new = adamw(weight[:, cols], grad, moment[:, cols], second[:, cols])
            for ref, value in zip(outs, (grad,) + new):
                ref[:, cols] = value


def adam_large(grad, in_state, out_state):
    shapes = [a.shape for a in (in_state[0],) * 4 + (out_state[0],) * 4]
    return pl.pallas_call(
        adam_kernel,
        in_specs=[pl.BlockSpec(memory_space=pltpu.VMEM)] * 7,
        out_specs=[pl.BlockSpec(memory_space=pltpu.VMEM)] * 8,
        out_shape=[jax.ShapeDtypeStruct(shape, jnp.float32) for shape in shapes],
        name="adam_large",
    )(grad, *in_state, *out_state)


def adamw(weight, grad, moment, second):
    moment_new = BETA_ONE * moment + (1.0 - BETA_ONE) * grad
    second_new = BETA_TWO * second + (1.0 - BETA_TWO) * grad * grad
    update = (
        moment_new
        / (1.0 - BETA_ONE**STEP)
        / (jnp.sqrt(second_new / (1.0 - BETA_TWO**STEP)) + ADAM_EPS)
    )
    return (weight - LEARN_RATE * (update + WEIGHT_DECAY * weight), moment_new, second_new)


def on_device(
    block_input,
    cotangent,
    seq_valid,
    in_weight,
    out_weight,
    small_params,
    in_moment,
    in_second,
    out_moment,
    out_second,
    small_moment,
    small_second,
):
    gain_in, beta_weight, conv_taps, decay_log, out_gain = split_small(small_params)
    replicas, shards = lax.axis_size("rep"), lax.axis_size("fsdp")
    shard_rows, in_cols = in_weight.shape
    blocks = gather_weights(replicas, shards, in_weight, out_weight)
    lanes = 128
    (
        block_output,
        input_grad,
        grads,
        d_gain_in,
        d_beta_weight,
        d_conv,
        d_decay,
        d_gain_out,
    ) = local_step(
        seq_valid,
        block_input,
        cotangent,
        blocks.reshape(shards, -1, shard_rows, blocks.shape[-1]),
        gain_in[None],
        jnp.pad(beta_weight, ((0, 0), (0, lanes - 2 * H))),
        conv_taps,
        jnp.pad(decay_log[None], ((0, 0), (H, lanes - 2 * H))),
        out_gain[None],
        in_cols,
    )
    small_local = jnp.concatenate(
        [
            d_gain_in[0],
            d_beta_weight[:, : 2 * H].reshape(-1),
            d_conv.reshape(-1),
            d_decay[0, H : 2 * H],
            d_gain_out[0],
        ]
    )
    count = small_local.shape[0]
    unit = 8 * replicas * lanes
    padded = jnp.pad(small_local, (0, -count % unit))
    grad, small_sum = reduce_grads(
        replicas,
        shards,
        grads.reshape(shards, -1, lanes),
        padded.reshape(1, -1, lanes),
    )
    small_grad = small_sum.reshape(-1)[:count]
    in_grad, new_in, in_m, in_v, out_grad, new_out, out_m, out_v = adam_large(
        grad, (in_weight, in_moment, in_second), (out_weight, out_moment, out_second)
    )
    new_small, small_m, small_v = adamw(small_params, small_grad, small_moment, small_second)
    return (
        block_output,
        input_grad,
        in_grad,
        out_grad,
        small_grad,
        new_in,
        new_out,
        new_small,
        in_m,
        in_v,
        out_m,
        out_v,
        small_m,
        small_v,
    )


def solution(mesh):
    in_specs = (
        P(("rep", "fsdp"), None, None),
        P(("rep", "fsdp"), None, None),
        P(("rep", "fsdp")),
        P("fsdp", None),
        P("fsdp", None),
        P(),
        P("fsdp", None),
        P("fsdp", None),
        P("fsdp", None),
        P("fsdp", None),
        P(),
        P(),
    )
    out_specs = (
        P(("rep", "fsdp"), None, None),
        P(("rep", "fsdp"), None, None),
        P("fsdp", None),
        P("fsdp", None),
        P(),
        P("fsdp", None),
        P("fsdp", None),
        P(),
        P("fsdp", None),
        P("fsdp", None),
        P("fsdp", None),
        P("fsdp", None),
        P(),
        P(),
    )
    return jax.shard_map(
        on_device, mesh=mesh, in_specs=in_specs, out_specs=out_specs, check_vma=False
    )
```

```python
import functools

import jax
import jax.numpy as jnp
from jax import lax
from jax.experimental import pallas as pl
from jax.experimental.pallas import tpu as pltpu
from jax.sharding import PartitionSpec as P

D = 512
H = 2
DK = 128
DV = 256
CONV = 4
CHUNK = 128
GATHER_GROUPS = 4
REDUCE_GROUPS = 8
MESH = pl.DeviceIdType.MESH
STEP = 3


EPS_NORM = 1e-06
BETA_ONE = 0.9
BETA_TWO = 0.95
ADAM_EPS = 1e-08
LEARN_RATE = 0.01
WEIGHT_DECAY = 0.1


def split_small(small):
    channels = 2 * H * DK + H * DV
    first = D
    second = first + D * 2 * H
    third = second + CONV * channels
    fourth = third + H
    return (
        small[:first],
        small[first:second].reshape(D, 2 * H),
        small[second:third].reshape(CONV, channels),
        small[third:fourth],
        small[fourth:],
    )


def split(value):
    high = value.astype(jnp.bfloat16)
    return (high, (value - high.astype(jnp.float32)).astype(jnp.bfloat16))


def dot(left, right, left_dim=1, right_dim=0):
    return lax.dot_general(
        left,
        right,
        (((left_dim,), (right_dim,)), ((), ())),
        preferred_element_type=jnp.float32,
    )


def dot3(left, right, left_dim=1, right_dim=0):
    return (
        dot(left[0], right[1], left_dim, right_dim)
        + dot(left[1], right[0], left_dim, right_dim)
    ) + dot(left[0], right[0], left_dim, right_dim)


def row_sum(value):
    return jnp.sum(value, axis=1, keepdims=True)


def col_sum(value):
    return jnp.sum(value, axis=0, keepdims=True)


def sigmoid(value):
    return 1.0 / (1.0 + jnp.exp(-value))


def total(*terms):
    out = None
    for term in terms:
        if term is not None:
            out = term if out is None else out + term
    return out


def unit_inverse(strict, levels, level_masks):
    size = strict[0].shape[0]
    rows = lax.broadcasted_iota(jnp.int32, (size, size), 0)
    cols = lax.broadcasted_iota(jnp.int32, (size, size), 1)
    eye = jnp.where(rows == cols, 1.0, 0.0)
    inverses = [eye - jnp.where(level_masks[0], a, 0.0) for a in strict]
    for level in range(1, levels):
        for n, a in enumerate(strict):
            inv = split(inverses[n])
            inner = dot3(inv, split(jnp.where(level_masks[level], a, 0.0)))
            inverses[n] = inverses[n] - dot3(split(inner), inv)
    return inverses


def local_kernel(
    flag_ref,
    x_ref,
    cot_ref,
    blocks_ref,
    gain_ref,
    bw_ref,
    taps_ref,
    dlog_ref,
    ogain_ref,
    out_ref,
    xgrad_ref,
    grad_ref,
    dgain_ref,
    dbw_ref,
    dtaps_ref,
    ddlog_ref,
    dogain_ref,
    proj_ref,
    conv_ref,
    mixed_ref,
    dproj_ref,
    dact_ref,
    win_ref,
    wout_ref,
    *,
    seqs,
):
    f32, bf16 = jnp.float32, jnp.bfloat16
    length, width = x_ref.shape[1:]
    channels = taps_ref.shape[1]
    lanes = bw_ref.shape[1]
    chunk = CHUNK if length % CHUNK == 0 else length
    chunks = length // chunk

    def keep(ref, value):
        if seqs == 1:
            ref[...] = value
        else:

            @pl.when(pl.program_id(0) == 0)
            def _():
                ref[...] = value

            @pl.when(pl.program_id(0) > 0)
            def _():
                ref[...] = ref[...] + value

    shards, col_blocks, shard_rows, block = blocks_ref.shape
    in_blocks = win_ref.shape[1] // block
    out_blocks = wout_ref.shape[1] // block
    for s in range(shards):
        here = slice(s * shard_rows, (s + 1) * shard_rows)
        for b in range(in_blocks):
            win_ref[here, b * block : (b + 1) * block] = blocks_ref[s, b]
        for b in range(out_blocks):
            wout_ref[here, b * block : (b + 1) * block] = blocks_ref[s, in_blocks + b]

    def keep_blocks(value, first):
        for s in range(shards):
            here = slice(s * shard_rows, (s + 1) * shard_rows)
            for b in range(value.shape[1] // block):
                keep(grad_ref.at[s, first + b], value[here, b * block : (b + 1) * block])

    gain = gain_ref[...]
    x = x_ref[0].astype(f32)
    x_scale = lax.rsqrt(jnp.mean(x * x, axis=1, keepdims=True) + EPS_NORM)
    x_hat = x * x_scale
    normed = x_hat * gain
    normed_bf = normed.astype(bf16)
    normed_s = (normed_bf, (normed - normed_bf.astype(f32)).astype(bf16))
    proj_ref[...] = dot(normed_bf, win_ref[...])
    bw_s = split(bw_ref[...])
    gate = dot3(normed_s, bw_s)
    gate_sig = sigmoid(gate)
    decay_rate = -jnp.exp(dlog_ref[...])
    softplus = jnp.maximum(gate, 0.0) + jnp.log1p(jnp.exp(-jnp.abs(gate)))
    log_decay = decay_rate * softplus

    row_id = lax.broadcasted_iota(jnp.int32, (length, DK), 0)

    def shifted(value, by):
        if by == 0:
            return value
        rolled = pltpu.roll(value, by % length, axis=0)
        if by > 0:
            return jnp.where(row_id >= by, rolled, 0.0)
        return jnp.where(row_id < length + by, rolled, 0.0)

    def conv_block(at):
        piece = proj_ref[:, at : at + DK]
        acc = None
        for tap in range(CONV):
            term = taps_ref[tap : tap + 1, at : at + DK] * shifted(piece, CONV - 1 - tap)
            acc = term if acc is None else acc + term
        return acc

    for at in range(0, channels, DK):
        conv_ref[:, at : at + DK] = conv_block(at)

    def active(at, wide):
        value = conv_ref[:, at : at + wide]
        return value * sigmoid(value)

    rows = lax.broadcasted_iota(jnp.int32, (chunk, chunk), 0)
    cols = lax.broadcasted_iota(jnp.int32, (chunk, chunk), 1)
    lower_strict = rows > cols
    lower_incl = rows >= cols
    ones_lower = jnp.where(lower_incl, 1.0, 0.0).astype(bf16)
    levels = chunk.bit_length() - 1
    level_masks = [
        ((rows >> level) ^ (cols >> level)) == 1 for level in range(levels)
    ]

    def exact_sum(value, dim):
        high = value.astype(bf16)
        rest = value - high.astype(f32)
        mid = rest.astype(bf16)
        low = (rest - mid.astype(f32)).astype(bf16)
        return (
            dot(ones_lower, low, dim, 0) + dot(ones_lower, mid, dim, 0)
        ) + dot(ones_lower, high, dim, 0)

    cums = [exact_sum(log_decay[c * chunk : (c + 1) * chunk], 1) for c in range(chunks)]
    cums_t = [jnp.transpose(cum) for cum in cums]

    scale = DK ** (-0.5)
    q_hat, q_rs, k_hat, k_rs, vals = ([], [], [], [], [])
    for h in range(H):
        q = active(h * DK, DK)
        k = active((H + h) * DK, DK)
        q_rs.append(lax.rsqrt(row_sum(q * q) + EPS_NORM))
        k_rs.append(lax.rsqrt(row_sum(k * k) + EPS_NORM))
        q_hat.append(q * q_rs[h])
        k_hat.append(k * k_rs[h])
        vals.append(active(2 * H * DK + h * DV, DV))

    units = [(h, c) for h in range(H) for c in range(chunks)]
    info = {}
    for h, c in units:
        span = slice(c * chunk, (c + 1) * chunk)
        k = k_hat[h][span]
        q = q_hat[h][span] * scale
        u = {"k": k, "q": q, "ks": split(k), "qs": split(q), "v": vals[h][span]}
        u["beta"] = gate_sig[span, h : h + 1]
        g = cums[c][:, H + h : H + h + 1]
        g_row = cums_t[c][H + h : H + h + 1, :]
        spread = g - g_row
        u["incl"] = jnp.where(lower_incl, jnp.exp(jnp.where(lower_incl, spread, 0.0)), 0.0)
        u["strict"] = jnp.where(lower_strict, u["incl"], 0.0)
        u["eg"] = jnp.exp(g)
        last = g[chunk - 1 : chunk]
        u["elast"] = jnp.exp(last)
        u["tail"] = jnp.exp(last - g)
        u["a"] = u["beta"] * u["strict"] * dot3(u["ks"], u["ks"], 1, 1)
        u["p"] = split(u["incl"] * dot3(u["qs"], u["ks"], 1, 1))
        info[h, c] = u
    inverses = unit_inverse([info[n]["a"] for n in units], levels, level_masks)
    for n, inverse in zip(units, inverses):
        info[n]["t"] = split(inverse)

    state_out = {}
    for h in range(H):
        state = None
        for c in range(chunks):
            u = info[h, c]
            u["s"] = state
            u["ss"] = None if state is None else split(state)
            if state is None:
                u["e"] = u["v"]
            else:
                u["e"] = u["v"] - u["eg"] * dot3(u["ks"], u["ss"])
            delta = dot3(u["t"], split(u["beta"] * u["e"]))
            u["d"] = split(delta)
            o = dot3(u["p"], u["d"])
            if state is not None:
                o = o + u["eg"] * dot3(u["qs"], u["ss"])
            state_out[h, c] = o
            if c < chunks - 1:
                u["kd"] = split(u["k"] * u["tail"])
                update = dot3(u["kd"], u["d"], 0, 0)
                state = update if state is None else u["elast"] * state + update

    flag = flag_ref[pl.program_id(0)].astype(f32)
    upstream_f = cot_ref[0].astype(f32) * flag
    upstream = upstream_f.astype(bf16)
    ogain = ogain_ref[...]
    o_grads = {}
    d_ogain = None
    for h in range(H):
        o = jnp.concatenate([state_out[h, c] for c in range(chunks)], axis=0)
        o_rs = lax.rsqrt(jnp.mean(o * o, axis=1, keepdims=True) + EPS_NORM)
        o_hat = o * o_rs
        at = channels + h * DV
        z = proj_ref[:, at : at + DV]
        z_sig = sigmoid(z)
        z_act = z * z_sig
        gained = o_hat * ogain
        mixed_ref[:, h * DV : (h + 1) * DV] = (gained * z_act).astype(bf16)
        d_mixed = dot(upstream, wout_ref[h * DV : (h + 1) * DV, :], 1, 1)
        d_z = d_mixed * gained * (z_sig * (1.0 + z * (1.0 - z_sig)))
        dproj_ref[:, at : at + DV] = d_z.astype(bf16)
        d_gained = d_mixed * z_act
        d_ogain = total(d_ogain, col_sum(d_gained * o_hat))
        d_hat = d_gained * ogain
        d_o = o_rs * (d_hat - o_hat * jnp.mean(o_hat * d_hat, axis=1, keepdims=True))
        for c in range(chunks):
            o_grads[h, c] = d_o[c * chunk : (c + 1) * chunk]
    keep(dogain_ref, d_ogain)
    out_ref[0] = x + dot(mixed_ref[...], wout_ref[...])
    keep_blocks(dot(mixed_ref[...], upstream, 0, 0), in_blocks)

    d_beta_cols = {}
    d_cum_cols = {}
    for h in range(H):
        d_state = None
        d_q_parts, d_k_parts = ([None] * chunks, [None] * chunks)
        for c in reversed(range(chunks)):
            u = info[h, c]
            span = slice(c * chunk, (c + 1) * chunk)
            d_o = o_grads[h, c]
            d_os = split(d_o)
            d_d = dot3(u["p"], d_os, 0, 0)
            d_qk = split(u["incl"] * dot3(d_os, u["d"], 1, 1))
            d_q = dot3(d_qk, u["ks"])
            d_k_minus = dot3(d_qk, u["qs"], 0, 0)
            d_k_plus = None
            d_last = None
            new_d_state = None
            if d_state is not None:
                d_ss = split(d_state)
                d_kd = u["tail"] * dot3(u["d"], d_ss, 1, 1)
                d_d = d_d + dot3(u["kd"], d_ss)
                d_k_minus = d_k_minus + d_kd
                d_last = jnp.sum(row_sum(u["k"] * d_kd), axis=0, keepdims=True)
                if u["s"] is not None:
                    d_last = d_last + u["elast"] * jnp.sum(
                        row_sum(u["s"] * d_state), axis=0, keepdims=True
                    )
                    new_d_state = u["elast"] * d_state
            d_r = dot3(u["t"], split(d_d), 0, 0)
            d_rs = split(d_r)
            hold = split(-u["strict"] * dot3(d_rs, u["d"], 1, 1))
            hold_k = dot3(hold, u["ks"])
            d_beta = row_sum(d_r * u["e"]) + row_sum(u["k"] * hold_k)
            d_k_plus = u["beta"] * hold_k
            d_k_minus = d_k_minus + dot3(hold, split(u["beta"] * u["k"]), 0, 0)
            d_e = u["beta"] * d_r
            dact_ref[span, 2 * H * DK + h * DV : 2 * H * DK + (h + 1) * DV] = d_e
            if u["s"] is not None:
                d_os_g = split(u["eg"] * d_o)
                d_es_g = split(-u["eg"] * d_e)
                d_q = d_q + dot3(d_os_g, u["ss"], 1, 1)
                d_k_plus = d_k_plus + dot3(d_es_g, u["ss"], 1, 1)
                new_d_state = total(
                    new_d_state,
                    dot3(u["qs"], d_os_g, 0, 0),
                    dot3(u["ks"], d_es_g, 0, 0),
                )
            d_cum = row_sum(u["q"] * d_q + u["k"] * (d_k_plus - d_k_minus))
            if d_last is not None:
                tail_row = lax.broadcasted_iota(jnp.int32, (chunk, 1), 0) == chunk - 1
                d_cum = d_cum + jnp.where(tail_row, d_last, 0.0)
            d_beta_cols[h, c] = d_beta
            d_cum_cols[h, c] = d_cum
            d_q_parts[c] = d_q
            d_k_parts[c] = d_k_plus + d_k_minus
            d_state = new_d_state
        d_q = jnp.concatenate(d_q_parts, axis=0) * scale
        d_k = jnp.concatenate(d_k_parts, axis=0)
        dact_ref[:, h * DK : (h + 1) * DK] = q_rs[h] * (
            d_q - q_hat[h] * row_sum(q_hat[h] * d_q)
        )
        dact_ref[:, (H + h) * DK : (H + h + 1) * DK] = k_rs[h] * (
            d_k - k_hat[h] * row_sum(k_hat[h] * d_k)
        )

    lane = lax.broadcasted_iota(jnp.int32, (chunk, lanes), 1)
    d_gate_parts = []
    d_dlog = None
    for c in range(chunks):
        span = slice(c * chunk, (c + 1) * chunk)
        d_cum = jnp.zeros((chunk, lanes), f32)
        d_beta = jnp.zeros((chunk, lanes), f32)
        for h in range(H):
            d_cum = jnp.where(lane == H + h, d_cum_cols[h, c], d_cum)
            d_beta = jnp.where(lane == h, d_beta_cols[h, c], d_beta)
        d_log = exact_sum(d_cum, 0)
        d_dlog = total(d_dlog, col_sum(d_log * log_decay[span]))
        sig = gate_sig[span]
        d_gate_parts.append(d_beta * sig * (1.0 - sig) + d_log * decay_rate * sig)
    keep(ddlog_ref, d_dlog)
    d_gate = jnp.concatenate(d_gate_parts, axis=0)
    d_gate_s = split(d_gate)
    keep(dbw_ref, dot3(normed_s, d_gate_s, 0, 0))

    d_taps = []
    for at in range(0, channels, DK):
        conv = conv_ref[:, at : at + DK]
        sig = sigmoid(conv)
        d_conv = dact_ref[:, at : at + DK] * (sig * (1.0 + conv * (1.0 - sig)))
        piece = proj_ref[:, at : at + DK]
        d_piece = None
        tap_rows = []
        for tap in range(CONV):
            by = CONV - 1 - tap
            tap_rows.append(col_sum(d_conv * shifted(piece, by)))
            d_piece = total(
                d_piece, taps_ref[tap : tap + 1, at : at + DK] * shifted(d_conv, -by)
            )
        dproj_ref[:, at : at + DK] = d_piece.astype(bf16)
        d_taps.append(jnp.concatenate(tap_rows, axis=0))
    keep(dtaps_ref, jnp.concatenate(d_taps, axis=1))

    keep_blocks(dot(normed_bf, dproj_ref[...], 0, 0), 0)
    d_normed = dot(dproj_ref[...], win_ref[...], 1, 1) + dot3(d_gate_s, bw_s, 1, 1)
    keep(dgain_ref, col_sum(d_normed * x_hat))
    d_hat = d_normed * gain
    d_x = x_scale * (d_hat - x_hat * jnp.mean(x_hat * d_hat, axis=1, keepdims=True))
    xgrad_ref[0] = upstream.astype(f32) + d_x


def local_step(
    seq_valid, block_input, cotangent, blocks, gain, bw, taps, dlog, ogain, in_cols
):
    seqs, length, width = block_input.shape
    shards, col_blocks, shard_rows, block = blocks.shape
    out_cols = col_blocks * block - in_cols
    channels = taps.shape[1]
    f32 = jnp.float32
    token = pl.BlockSpec((1, length, width), lambda i: (i, 0, 0))

    def whole(shape):
        return pl.BlockSpec(shape, lambda i: (0,) * len(shape))

    sums = [blocks.shape, gain.shape, bw.shape, taps.shape, dlog.shape, ogain.shape]
    return pl.pallas_call(
        functools.partial(local_kernel, seqs=seqs),
        grid=(seqs,),
        in_specs=[pl.BlockSpec(memory_space=pltpu.SMEM), token, token]
        + [whole(shape) for shape in sums],
        out_specs=[token, token] + [whole(shape) for shape in sums],
        out_shape=[jax.ShapeDtypeStruct(block_input.shape, f32)] * 2
        + [jax.ShapeDtypeStruct(shape, f32) for shape in sums],
        scratch_shapes=[
            pltpu.VMEM((length, in_cols), f32),
            pltpu.VMEM((length, channels), f32),
            pltpu.VMEM((length, H * DV), jnp.bfloat16),
            pltpu.VMEM((length, in_cols), jnp.bfloat16),
            pltpu.VMEM((length, channels), f32),
            pltpu.VMEM((shards * shard_rows, in_cols), jnp.bfloat16),
            pltpu.VMEM((shards * shard_rows, out_cols), jnp.bfloat16),
        ],
        compiler_params=pltpu.CompilerParams(
            dimension_semantics=("arbitrary",), vmem_limit_bytes=60 * 1024 * 1024
        ),
        name="local_step",
    )(seq_valid, block_input, cotangent, blocks, gain, bw, taps, dlog, ogain)


def greet(replicas, shards):
    rep, shard = lax.axis_index("rep"), lax.axis_index("fsdp")
    barrier = pltpu.get_barrier_semaphore()
    bits = replicas.bit_length() - 1
    for bit in range(bits):
        pl.semaphore_signal(
            barrier, inc=1, device_id=(flip(rep, bit), shard), device_id_type=MESH
        )
    for step in range(1, shards):
        pl.semaphore_signal(
            barrier,
            inc=1,
            device_id=(rep, lax.rem(shard + step, shards)),
            device_id_type=MESH,
        )
    pl.semaphore_wait(barrier, bits + shards - 1)


def bit_of(rep, bit):
    return lax.rem(rep // (1 << bit), 2)


def flip(rep, bit):
    return rep + (1 << bit) * (1 - 2 * bit_of(rep, bit))


def bit_orders(replicas, groups):
    bits = list(range(replicas.bit_length() - 1))
    orders = (bits, bits[:1] + bits[1:][::-1])
    return [orders[g % 2] for g in range(groups)]


def group_count(rows, replicas, tile, most):
    while most > 1 and rows % (most * replicas * tile):
        most //= 2
    return most


def aligned(offset, size):
    return pl.ds(pl.multiple_of(offset, size), size)


class Copies:
    def __init__(self, send_sems, recv_sems):
        self.send_sems, self.recv_sems, self.started = send_sems, recv_sems, []

    def start(self, src, dst, rep, shard):
        at = len(self.started)
        copy = pltpu.make_async_remote_copy(
            src_ref=src,
            dst_ref=dst,
            send_sem=self.send_sems.at[at],
            recv_sem=self.recv_sems.at[at],
            device_id=(rep, shard),
            device_id_type=MESH,
        )
        copy.start()
        self.started.append(copy)
        return copy

    def finish(self):
        for copy in self.started:
            copy.wait_send()


def gather_kernel(replicas, shards, win_ref, wout_ref, full_ref, mine_ref, send_sems, recv_sems):
    rep, shard = lax.axis_index("rep"), lax.axis_index("fsdp")
    rows, block = win_ref.shape[0], full_ref.shape[-1]
    at = 0
    for ref in (win_ref, wout_ref):
        for b in range(ref.shape[1] // block):
            value = ref[:, b * block : (b + 1) * block].astype(jnp.bfloat16)
            mine_ref[at : at + rows, :] = value
            at += rows
    full_ref[shard] = mine_ref[...]
    greet(replicas, shards)
    copies = Copies(send_sems, recv_sems)
    total_rows = mine_ref.shape[0]
    orders = bit_orders(replicas, group_count(total_rows, replicas, 16, GATHER_GROUPS))
    span = total_rows // len(orders)
    state = []
    for g, order in enumerate(orders):
        size, base = span, g * span
        for bit in order:
            size //= 2
            base = base + bit_of(rep, bit) * size
        pending = []
        for step in range(1, shards):
            pending.append(
                copies.start(
                    mine_ref.at[aligned(base, size), :],
                    full_ref.at[shard, aligned(base, size), :],
                    rep,
                    lax.rem(shard + step, shards),
                )
            )
        state.append([base, size, pending])
    for level in range(len(orders[0])):
        for g, order in enumerate(orders):
            base, size, pending = state[g]
            for copy in pending:
                copy.wait_recv()
            bit = order[len(order) - 1 - level]
            here = full_ref.at[:, aligned(base, size), :]
            pending = [copies.start(here, here, flip(rep, bit), shard)]
            state[g] = [base - bit_of(rep, bit) * size, 2 * size, pending]
    for _, _, pending in state:
        for copy in pending:
            copy.wait_recv()
    copies.finish()


def gather_weights(replicas, shards, in_weight, out_weight):
    rows, block = in_weight.shape[0], 128
    total_rows = rows * (in_weight.shape[1] + out_weight.shape[1]) // block
    bits = replicas.bit_length() - 1
    groups = group_count(total_rows, replicas, 16, GATHER_GROUPS)
    count = groups * (bits + shards - 1)
    return pl.pallas_call(
        functools.partial(gather_kernel, replicas, shards),
        in_specs=[pl.BlockSpec(memory_space=pltpu.VMEM)] * 2,
        out_specs=pl.BlockSpec(memory_space=pltpu.VMEM),
        out_shape=jax.ShapeDtypeStruct((shards, total_rows, block), jnp.bfloat16),
        scratch_shapes=[
            pltpu.VMEM((total_rows, block), jnp.bfloat16),
            pltpu.SemaphoreType.DMA((count,)),
            pltpu.SemaphoreType.DMA((count,)),
        ],
        compiler_params=pltpu.CompilerParams(
            collective_id=0, has_side_effects=True, vmem_limit_bytes=24 * 1024 * 1024
        ),
        name="gather_weights",
    )(in_weight, out_weight)


def reduce_kernel(replicas, shards, grad_ref, small_ref, out_ref, small_out_ref, *scratch):
    rep, shard = lax.axis_index("rep"), lax.axis_index("fsdp")
    send_sems, recv_sems = scratch[-2:]
    count = group_count(grad_ref.shape[1], replicas, 8, REDUCE_GROUPS)
    orders = bit_orders(replicas, count + 1)
    bits = len(orders[0])
    copies = Copies(send_sems, recv_sems)
    greet(replicas, shards)
    span = grad_ref.shape[1] // count
    groups = []
    for g in range(count + 1):
        bufs = scratch[g * (bits + 1) : (g + 1) * (bits + 1)]
        if g < count:
            groups.append([grad_ref, out_ref, g * span, span, orders[g], bufs])
        else:
            groups.append(
                [small_ref, small_out_ref, 0, small_ref.shape[1], orders[0], bufs]
            )

    def halve(group, level):
        cur, _, base, size, order, bufs = group
        half = size // 2
        mine = bit_of(rep, order[level])
        there = base + (1 - mine) * half
        copy = copies.start(
            cur.at[:, aligned(there, half), :], bufs[level], flip(rep, order[level]), shard
        )
        return copy, base + mine * half, half

    live = [halve(group, 0) for group in groups]
    for level in range(bits):
        for g, group in enumerate(groups):
            copy, mine, half = live[g]
            cur, bufs = group[0], group[5]
            copy.wait_recv()
            bufs[level][...] = bufs[level][...] + cur[:, aligned(mine, half), :]
            group[0], group[2], group[3] = bufs[level], 0, half
            if level + 1 < bits:
                live[g] = halve(group, level + 1)
            else:
                pending = []
                for step in range(1, shards):
                    to = lax.rem(shard + step, shards)
                    if g < count:
                        src, slot = group[0].at[to], bufs[bits].at[step - 1]
                    else:
                        src, slot = group[0].at[0], bufs[bits].at[shard]
                    pending.append(copies.start(src, slot, rep, to))
                live[g] = pending
    spread = []
    for g, group in enumerate(groups):
        cur, out, _, size, order, bufs = group
        base = g * span if g < count else 0
        full = span if g < count else small_ref.shape[1]
        for bit in order:
            full //= 2
            base = base + bit_of(rep, bit) * full
        if g == count:
            bufs[bits][shard] = cur[0]
        for copy in live[g]:
            copy.wait_recv()
        if g < count:
            value = cur[shard]
            for step in range(1, shards):
                value = value + bufs[bits][step - 1]
        else:
            value = bufs[bits][0]
            for s in range(1, shards):
                value = value + bufs[bits][s]
        out[aligned(base, size), :] = value
        spread.append([base, size, None])
        start_spread(copies, out, spread[g], order[-1], rep, shard)
    for level in range(1, bits + 1):
        for g, group in enumerate(groups):
            spread[g][2].wait_recv()
            if level < bits:
                start_spread(
                    copies, group[1], spread[g], group[4][bits - 1 - level], rep, shard
                )
    copies.finish()


def start_spread(copies, out, state, bit, rep, shard):
    base, size, _ = state
    here = out.at[aligned(base, size), :]
    copy = copies.start(here, here, flip(rep, bit), shard)
    state[:] = [base - bit_of(rep, bit) * size, 2 * size, copy]


def reduce_grads(replicas, shards, grads, small):
    rows, block = grads.shape[1:]
    bits = replicas.bit_length() - 1
    groups = group_count(rows, replicas, 8, REDUCE_GROUPS)
    scratch = []
    for g in range(groups + 1):
        parts, size = (shards, rows // groups) if g < groups else (1, small.shape[1])
        for _ in range(bits):
            size //= 2
            scratch.append(pltpu.VMEM((parts, size, block), jnp.float32))
        slots = shards - 1 if g < groups else shards
        scratch.append(pltpu.VMEM((slots, size, block), jnp.float32))
    count = (groups + 1) * (2 * bits + shards - 1)
    return pl.pallas_call(
        functools.partial(reduce_kernel, replicas, shards),
        in_specs=[pl.BlockSpec(memory_space=pltpu.VMEM)] * 2,
        out_specs=[pl.BlockSpec(memory_space=pltpu.VMEM)] * 2,
        out_shape=[
            jax.ShapeDtypeStruct((rows, block), jnp.float32),
            jax.ShapeDtypeStruct(small.shape[1:], jnp.float32),
        ],
        scratch_shapes=scratch
        + [pltpu.SemaphoreType.DMA((count,)), pltpu.SemaphoreType.DMA((count,))],
        compiler_params=pltpu.CompilerParams(
            collective_id=1, has_side_effects=True, vmem_limit_bytes=40 * 1024 * 1024
        ),
        name="reduce_grads",
    )(grads, small)


def adam_kernel(grad_ref, *refs):
    rows, block = refs[0].shape[0], grad_ref.shape[1]
    at = 0
    for first in (0, 3):
        weight, moment, second = refs[first : first + 3]
        outs = refs[6 + 4 * (first // 3) : 10 + 4 * (first // 3)]
        for b in range(weight.shape[1] // block):
            cols = slice(b * block, (b + 1) * block)
            grad = grad_ref[at : at + rows, :]
            at += rows
            new = adamw(weight[:, cols], grad, moment[:, cols], second[:, cols])
            for ref, value in zip(outs, (grad,) + new):
                ref[:, cols] = value


def adam_large(grad, in_state, out_state):
    shapes = [a.shape for a in (in_state[0],) * 4 + (out_state[0],) * 4]
    return pl.pallas_call(
        adam_kernel,
        in_specs=[pl.BlockSpec(memory_space=pltpu.VMEM)] * 7,
        out_specs=[pl.BlockSpec(memory_space=pltpu.VMEM)] * 8,
        out_shape=[jax.ShapeDtypeStruct(shape, jnp.float32) for shape in shapes],
        name="adam_large",
    )(grad, *in_state, *out_state)


def adamw(weight, grad, moment, second):
    moment_new = BETA_ONE * moment + (1.0 - BETA_ONE) * grad
    second_new = BETA_TWO * second + (1.0 - BETA_TWO) * grad * grad
    update = (
        moment_new
        / (1.0 - BETA_ONE**STEP)
        / (jnp.sqrt(second_new / (1.0 - BETA_TWO**STEP)) + ADAM_EPS)
    )
    return (weight - LEARN_RATE * (update + WEIGHT_DECAY * weight), moment_new, second_new)


def on_device(
    block_input,
    cotangent,
    seq_valid,
    in_weight,
    out_weight,
    small_params,
    in_moment,
    in_second,
    out_moment,
    out_second,
    small_moment,
    small_second,
):
    gain_in, beta_weight, conv_taps, decay_log, out_gain = split_small(small_params)
    replicas, shards = lax.axis_size("rep"), lax.axis_size("fsdp")
    shard_rows, in_cols = in_weight.shape
    blocks = gather_weights(replicas, shards, in_weight, out_weight)
    lanes = 128
    (
        block_output,
        input_grad,
        grads,
        d_gain_in,
        d_beta_weight,
        d_conv,
        d_decay,
        d_gain_out,
    ) = local_step(
        seq_valid,
        block_input,
        cotangent,
        blocks.reshape(shards, -1, shard_rows, blocks.shape[-1]),
        gain_in[None],
        jnp.pad(beta_weight, ((0, 0), (0, lanes - 2 * H))),
        conv_taps,
        jnp.pad(decay_log[None], ((0, 0), (H, lanes - 2 * H))),
        out_gain[None],
        in_cols,
    )
    small_local = jnp.concatenate(
        [
            d_gain_in[0],
            d_beta_weight[:, : 2 * H].reshape(-1),
            d_conv.reshape(-1),
            d_decay[0, H : 2 * H],
            d_gain_out[0],
        ]
    )
    count = small_local.shape[0]
    unit = 8 * replicas * lanes
    padded = jnp.pad(small_local, (0, -count % unit))
    grad, small_sum = reduce_grads(
        replicas,
        shards,
        grads.reshape(shards, -1, lanes),
        padded.reshape(1, -1, lanes),
    )
    small_grad = small_sum.reshape(-1)[:count]
    in_grad, new_in, in_m, in_v, out_grad, new_out, out_m, out_v = adam_large(
        grad, (in_weight, in_moment, in_second), (out_weight, out_moment, out_second)
    )
    new_small, small_m, small_v = adamw(small_params, small_grad, small_moment, small_second)
    return (
        block_output,
        input_grad,
        in_grad,
        out_grad,
        small_grad,
        new_in,
        new_out,
        new_small,
        in_m,
        in_v,
        out_m,
        out_v,
        small_m,
        small_v,
    )


def solution(mesh):
    in_specs = (
        P(("rep", "fsdp"), None, None),
        P(("rep", "fsdp"), None, None),
        P(("rep", "fsdp")),
        P("fsdp", None),
        P("fsdp", None),
        P(),
        P("fsdp", None),
        P("fsdp", None),
        P("fsdp", None),
        P("fsdp", None),
        P(),
        P(),
    )
    out_specs = (
        P(("rep", "fsdp"), None, None),
        P(("rep", "fsdp"), None, None),
        P("fsdp", None),
        P("fsdp", None),
        P(),
        P("fsdp", None),
        P("fsdp", None),
        P(),
        P("fsdp", None),
        P("fsdp", None),
        P("fsdp", None),
        P("fsdp", None),
        P(),
        P(),
    )
    return jax.shard_map(
        on_device, mesh=mesh, in_specs=in_specs, out_specs=out_specs, check_vma=False
    )
```
